32 devices in a mesh: groups: 2 (over y), ctx: 16 (over z, x, core).
Axes of the slice: x: 2, y: 2, z: 4, core: 2. Of those that a mesh axis runs over, the one named last changes fastest.
Arguments:
- x_in: bfloat16 [4096, 8192], P(('groups', 'ctx')), parts along dimension 0, may hold values from -6 to 6
- bc_in: bfloat16 [4096, 2048], P(('groups', 'ctx')), parts along dimension 0, may hold values from -6 to 6
- z_in: bfloat16 [4096, 8192], P(('groups', 'ctx')), parts along dimension 0, may hold values from -6 to 6
- dt_in: bfloat16 [4096, 128], P(('groups', 'ctx')), parts along dimension 0, may hold values from -4 to 4
- conv_x: float32 [4, 8192], replicated, may hold values from -3 to 3
- conv_bc: float32 [4, 2048], replicated, may hold values from -3 to 3
- dt_bias: float32 [128], replicated, may hold values from -6 to -3
- a_rate: float32 [128], replicated, may hold values from 0.001953125 to 1
- d_skip: float32 [128], replicated, may hold values from 0.5 to 2
- gain: float32 [8192], replicated, may hold values from 0.5 to 1.5
Outputs:
- mixed: bfloat16 [4096, 8192], P(('groups', 'ctx')), parts along dimension 0
The draws below stay inside these ranges and needn't reach their ends.
There are 2 independent parts, one for each index of `groups`. The reference program is written for one: setup_inputs(seed, part) draws one part's arguments, and reference() takes and returns one part's arrays. A program takes and returns all parts, laid end to end along the dimension named above; an argument that names none is the same for every part. Nothing has to cross between parts.
All inputs are finite; a program needn't handle non-finite values.
Results may differ from the reference program's by a relative error of at most 0.001.
Values may be sent and summed in bfloat16 or wider, within the bound.
No kernel may reach another device: no remote copies, remote signals or barrier semaphores. Data moves between devices by JAX's collectives and lax.ppermute only.
A program may use at most 64 MiB of HBM per device.

```python
import math
import jax
import jax.numpy as jnp
from jax import lax

HEADS = 128
HEAD_DIM = 64
STATE = 128
GROUPS = 8
CONV = 4
TOK_DEV = 128
LENGTH = 2048


def block_levels(own_key, extent, pieces, smallest, top_value):
    def one(axis_at, blocks):
        heights = jax.random.uniform(jax.random.fold_in(jax.random.fold_in(own_key, 6), axis_at), (blocks,), jnp.float32, smallest / len(pieces), top_value / len(pieces))
        return jnp.repeat(jnp.exp(heights), extent[axis_at] // blocks).reshape((-1,) + (1,) * (len(extent) - axis_at - 1))

    level = one(*pieces[0])
    for cut in pieces[1:]:
        level = level * one(*cut)
    return level


def noise(key, extent, spread, bound, shards=(), held_as=jnp.bfloat16):
    entries = spread * jax.random.normal(key, extent, jnp.float32)
    if shards:
        entries = entries * block_levels(key, extent, shards, -0.22, 0.18)
    return jnp.clip(entries, -bound, bound).astype(held_as)


def setup_inputs(seed: int = 0, part: int = 0) -> dict:
    arg_keys = jax.random.split(jax.random.key(seed), 11)
    own_keys = jax.random.split(jax.random.fold_in(arg_keys[10], part), 11)
    return {
        "x_in": noise(own_keys[0], (LENGTH, HEADS * HEAD_DIM), 1.0, 6.0, ((0, 16),)),
        "bc_in": noise(own_keys[1], (LENGTH, 2 * GROUPS * STATE), 1.0, 6.0, ((0, 16),)),
        "z_in": noise(own_keys[2], (LENGTH, HEADS * HEAD_DIM), 1.0, 6.0, ((0, 16),)),
        "dt_in": noise(own_keys[3], (LENGTH, HEADS), 1.0, 4.0, ((0, 16),)),
        "conv_x": noise(arg_keys[4], (CONV, HEADS * HEAD_DIM), 0.5, 3.0, (), jnp.float32),
        "conv_bc": noise(arg_keys[5], (CONV, 2 * GROUPS * STATE), 0.5, 3.0, (), jnp.float32),
        "dt_bias": jnp.clip(jax.random.uniform(arg_keys[6], (HEADS,), jnp.float32, -6.0, -3.0), -6.0, -3.0),
        "a_rate": jnp.clip(jnp.exp(jax.random.uniform(arg_keys[7], (HEADS,), jnp.float32, math.log(0.001953125), math.log(1.0))), 0.001953125, 1.0),
        "d_skip": jnp.clip(jax.random.uniform(arg_keys[8], (HEADS,), jnp.float32, 0.5, 2.0), 0.5, 2.0),
        "gain": jnp.clip(1.0 + 0.1 * jax.random.normal(arg_keys[9], (HEADS * HEAD_DIM,), jnp.float32), 0.5, 1.5),
    }


HIGH = lax.Precision.HIGHEST

def block_terms(xc, bcc, dt, a_rate, n_groups, n_state):
    rows, width = xc.shape
    heads = dt.shape[1]
    per = heads // n_groups
    hdim = width // heads
    bmat = bcc[:, :n_groups * n_state].reshape(rows, n_groups, n_state)
    cmat = bcc[:, n_groups * n_state:].reshape(rows, n_groups, n_state)
    cumg = jnp.cumsum(-dt * a_rate, axis=0).reshape(rows, n_groups, per)
    dtg = dt.reshape(rows, n_groups, per)
    xg = xc.reshape(rows, n_groups, per, hdim)
    scores = jnp.einsum('tgn,sgn->gts', cmat, bmat, precision=HIGH)
    cum_t = jnp.transpose(cumg, (1, 2, 0))
    diff = cum_t[:, :, :, None] - cum_t[:, :, None, :]
    posit = jnp.arange(rows)
    causal = posit[:, None] >= posit[None, :]
    decay = jnp.exp(jnp.where(causal[None, None], diff, -jnp.inf))
    dt_t = jnp.transpose(dtg, (1, 2, 0))
    weights = scores[:, None] * decay * dt_t[:, :, None, :]
    y_diag = jnp.einsum('gkts,sgkp->tgkp', weights, xg, precision=HIGH)
    tail = jnp.exp(cumg[-1] - cumg) * dtg
    s_loc = jnp.einsum('sgkp,sgn->gkpn', xg * tail[..., None], bmat, precision=HIGH)
    total = jnp.exp(cumg[-1])
    return (y_diag, s_loc, total, jnp.exp(cumg), cmat, xg)

def reference(x_in, bc_in, z_in, dt_in, conv_x, conv_bc, dt_bias, a_rate, d_skip, gain):
    length, width = x_in.shape
    heads = dt_bias.shape[0]
    hdim = width // heads
    per = heads // GROUPS
    joined = jnp.concatenate([x_in, bc_in], axis=1).astype(jnp.float32)
    padded = jnp.pad(joined, ((CONV - 1, 0), (0, 0)))
    taps = jnp.concatenate([conv_x, conv_bc], axis=1)
    mixed_in = taps[0] * padded[0:length]
    for k in range(1, CONV):
        mixed_in = mixed_in + taps[k] * padded[k:k + length]
    conv = jax.nn.silu(mixed_in)
    dt = jax.nn.softplus(dt_in.astype(jnp.float32) + dt_bias)
    blocks = length // TOK_DEV
    xcs = conv[:, :width].reshape(blocks, TOK_DEV, width)
    bccs = conv[:, width:].reshape(blocks, TOK_DEV, 2 * GROUPS * STATE)
    dts = dt.reshape(blocks, TOK_DEV, heads)

    def step(carry, item):
        xc, bcc, dtb = item
        y_diag, s_loc, total, ecum, cmat, xg = block_terms(xc, bcc, dtb, a_rate, GROUPS, STATE)
        y_off = jnp.einsum('tgn,gkpn->tgkp', cmat, carry, precision=HIGH) * ecum[..., None]
        dskip = d_skip.reshape(GROUPS, per)[None, :, :, None] * xg
        y = (y_diag + y_off + dskip).reshape(TOK_DEV, width)
        new = total[:, :, None, None] * carry + s_loc
        return (new, y)
    init = jnp.zeros((GROUPS, per, hdim, STATE), jnp.float32)
    final, ys = lax.scan(step, init, (xcs, bccs, dts))
    y = ys.reshape(length, width)
    gated = y * jax.nn.silu(z_in.astype(jnp.float32))
    grouped = gated.reshape(length, GROUPS, per * hdim)
    scale = lax.rsqrt(lax.optimization_barrier(jnp.mean(grouped * grouped, axis=-1, keepdims=True)) + 1e-05)
    return ((grouped * scale).reshape(length, width) * gain).astype(jnp.bfloat16)
```

```python
import functools

import jax
import jax.numpy as jnp
from jax import lax
from jax.experimental import pallas as pl
from jax.experimental.pallas import tpu as pltpu
from jax.sharding import PartitionSpec as P

STATE = 128
GROUPS = 8
EPS = 1e-05
F32, BF16 = jnp.float32, jnp.bfloat16
WIRE = jnp.float16
PEAK = 4 * 3.0 * 6.0
DT_TOP = 1.3133


def plane_size(n, groups):
    size = 1
    while (2 * size) ** 3 <= 4 * n and n % (2 * size) == 0 and groups % (2 * size) == 0:
        size *= 2
    return size


def silu(v):
    return v / (1.0 + jnp.exp(-v))


def split(v):
    hi = v.astype(BF16)
    return hi, (v - hi.astype(F32)).astype(BF16)


def mm(a, b, dims=((1,), (0,))):
    return lax.dot_general(a, b, (dims, ((), ())), preferred_element_type=F32)


def spread(v, e_ref):
    hi = v.astype(BF16)
    rest = v - hi.astype(F32)
    mid = rest.astype(BF16)
    low = (rest - mid.astype(F32)).astype(BF16)
    return mm(jnp.concatenate([hi, mid, low], axis=1), e_ref[...])


def conv_silu(x, halo, taps):
    rows = x.shape[0]
    count = taps.shape[0]
    xf = x.astype(F32)
    hf = halo.astype(F32)
    at = lax.broadcasted_iota(jnp.int32, (rows, 1), 0)
    total = taps[count - 1 : count] * xf
    for back in range(1, count):
        moved = pltpu.roll(xf, back, 0)
        for row in range(back):
            src = hf.shape[0] - back + row
            moved = jnp.where(at == row, hf[src : src + 1], moved)
        total = total + taps[count - 1 - back : count - back] * moved
    return silu(total)


def steps_kernel(dt_ref, bias_ref, rate_ref, skip_ref, tail_ref, cum_ref, row_ref, ecum_ref, tot_ref):
    groups, rows, per = tail_ref.shape
    v = dt_ref[...].astype(F32) + bias_ref[...]
    dt = jnp.maximum(v, 0.0) + jnp.log1p(jnp.exp(-jnp.abs(v)))
    cum = -rate_ref[...] * dt
    at = lax.broadcasted_iota(jnp.int32, cum.shape, 0)
    step = 1
    while step < rows:
        cum = cum + jnp.where(at >= step, pltpu.roll(cum, step, 0), 0.0)
        step *= 2
    total = cum[rows - 1 : rows]
    tot_ref[...] = total
    tail = jnp.exp(total - cum) * dt
    ecum = jnp.exp(cum)
    row = (jnp.log(dt) - cum).T
    for g in range(groups):
        cols = slice(g * per, (g + 1) * per)
        tail_ref[g] = tail[:, cols]
        cum_ref[g] = cum[:, cols]
        row_ref[g] = row[cols]
        ecum_ref[g, :rows] = ecum[:, cols]
        ecum_ref[g, rows:] = jnp.broadcast_to(skip_ref[:, cols], (8, per))


def state_kernel(order_ref, x_ref, xh_ref, tx_ref, b_ref, bh_ref, tb_ref, tail_ref, e_ref, s_ref, xc_ref):
    xc = conv_silu(x_ref[...], xh_ref[...], tx_ref[...])
    xc_ref[0] = xc
    b = conv_silu(b_ref[...], bh_ref[...], tb_ref[...])
    xt = xc * spread(tail_ref[0], e_ref)
    xhi, xlo = split(xt)
    bhi, blo = split(b)
    s = mm(jnp.concatenate([bhi, blo], axis=0), jnp.concatenate([xhi, xhi], axis=0), ((0,), (0,)))
    s_ref[0] = s + mm(bhi, xlo, ((0,), (0,)))


def local_kernel(order_ref, b_ref, bh_ref, tb_ref, c_ref, ch_ref, tc_ref, xc_ref, cum_ref, row_ref, ecum_ref, e_ref, z_ref, m1_ref, m2_ref, co_ref):
    rows = z_ref.shape[0]
    per = cum_ref.shape[2]
    hdim = z_ref.shape[1] // per
    b = conv_silu(b_ref[...], bh_ref[...], tb_ref[...])
    c = conv_silu(c_ref[...], ch_ref[...], tc_ref[...])
    co_ref[0] = c
    bhi, blo = split(b)
    chi, clo = split(c)
    last = ((1,), (1,))
    scores = mm(jnp.concatenate([chi, clo], axis=1), jnp.concatenate([bhi, bhi], axis=1), last) + mm(chi, blo, last)
    causal = lax.broadcasted_iota(jnp.int32, (rows, rows), 0) >= lax.broadcasted_iota(jnp.int32, (rows, rows), 1)
    wide = spread(ecum_ref[0], e_ref)
    z = silu(z_ref[...].astype(F32))
    m1_ref[0] = wide[:rows] * z
    skip = wide[rows : rows + 1]
    first = lax.broadcasted_iota(jnp.int32, (rows, 2 * hdim), 1) < hdim
    for pair in range(per // 2):
        cols = slice(pair * 2 * hdim, (pair + 1) * 2 * hdim)
        weights = []
        for h in (2 * pair, 2 * pair + 1):
            e = jnp.exp(cum_ref[0, :, h : h + 1] + row_ref[0, h : h + 1, :])
            weights.append(jnp.where(causal, e * scores, 0.0))
        w = jnp.concatenate(weights, axis=1)
        x = xc_ref[0, :, cols]
        xb = jnp.concatenate([jnp.where(first, x, 0.0), jnp.where(first, 0.0, x)], axis=0)
        whi, wlo = split(w)
        xhi, xlo = split(xb)
        y = mm(whi, xhi) + mm(wlo, xhi) + mm(whi, xlo)
        m2_ref[0, :, cols] = (y + skip[:, cols] * x) * z[:, cols]


def finish_kernel(order_ref, p_ref, c_ref, m1_ref, m2_ref, gain_ref, held_ref, out_ref):
    chi, clo = split(c_ref[0])
    phi, plo = split(p_ref[0])
    y = mm(jnp.concatenate([chi, clo], axis=1), jnp.concatenate([phi, phi], axis=0)) + mm(chi, plo)
    gated = m2_ref[0] + m1_ref[0] * y
    scale = lax.rsqrt(jnp.mean(gated * gated, axis=1, keepdims=True) + EPS)
    out_ref[...] = (gated * scale * gain_ref[...]).astype(BF16)


def call(body, order, out_shape, in_specs, out_specs, args, **more):
    grid_spec = pltpu.PrefetchScalarGridSpec(
        num_scalar_prefetch=1, grid=order.shape, in_specs=in_specs, out_specs=out_specs
    )
    return pl.pallas_call(body, out_shape=out_shape, grid_spec=grid_spec, **more)(order, *args)


def shards(x_in, bc_in, z_in, dt_in, conv_x, conv_bc, dt_bias, a_rate, d_skip, gain):
    rows, width = x_in.shape
    heads = dt_bias.shape[0]
    hdim = width // heads
    per = heads // GROUPS
    unit = per * hdim
    count = conv_x.shape[0]
    axis = "ctx"
    n = lax.axis_size(axis)
    plane = plane_size(n, GROUPS)
    planes = n // plane
    chunks = GROUPS // plane
    bits = plane.bit_length() - 1
    index = lax.axis_index(axis)
    j = index % plane
    z = index // plane
    scale = 2.0**-max(0, 1 + int(n * rows * DT_TOP * PEAK * PEAK / 65504.0).bit_length())

    def swap(v, bit):
        return lax.ppermute(v, axis, [(i, i ^ (1 << bit)) for i in range(n)])

    def send(v, move):
        return move((v * scale).astype(WIRE)).astype(F32) * (1.0 / scale)

    ends = jnp.concatenate([x_in[rows - (count - 1) :], bc_in[rows - (count - 1) :]], axis=1)
    rim = lax.ppermute(ends, axis, [(i, i + 1) for i in range(n - 1)])
    rim_x = rim[:, :width]
    rim_bc = rim[:, width:]

    small = [
        jax.ShapeDtypeStruct((GROUPS, rows, per), F32),
        jax.ShapeDtypeStruct((GROUPS, rows, per), F32),
        jax.ShapeDtypeStruct((GROUPS, per, rows), F32),
        jax.ShapeDtypeStruct((GROUPS, rows + 8, per), F32),
        jax.ShapeDtypeStruct((1, heads), F32),
    ]
    tail, cum, row, ecum, total = pl.pallas_call(steps_kernel, out_shape=small)(
        dt_in, dt_bias[None], a_rate[None], d_skip[None]
    )
    logs = total
    for bit in range(bits):
        logs = jnp.concatenate([logs, swap(logs, bit)], axis=0)

    head_map = (jnp.arange(unit)[None, :] // hdim == jnp.arange(per)[:, None]).astype(BF16)
    head_map = jnp.concatenate([head_map] * 3, axis=0)

    def flip(p):
        return int(format(p, f"0{bits}b")[::-1], 2) if bits else 0

    def orders(chunk, positions):
        return jnp.stack([(j ^ flip(p)) * chunks + chunk for p in positions]).astype(jnp.int32)

    def group_rows(log, order):
        values = jnp.exp(log).reshape(GROUPS, per)
        values = jnp.concatenate([lax.dynamic_slice_in_dim(values, order[k], 1, 0) for k in range(order.shape[0])], axis=0)
        return jnp.broadcast_to(values[:, :, None], (*values.shape, hdim)).reshape(values.shape[0], 1, unit)

    def at_group(shape, base=0):
        return pl.BlockSpec(shape, lambda s, o: (0, o[s] + base))

    def at_lead(shape):
        return pl.BlockSpec(shape, lambda s, o: (o[s], 0, 0))

    def in_set(shape):
        return pl.BlockSpec(shape, lambda s, o: (s, 0, 0))

    whole_map = pl.BlockSpec(head_map.shape, lambda s, o: (0, 0))

    def states(order):
        size = order.shape[0]
        return call(
            state_kernel,
            order,
            [jax.ShapeDtypeStruct((size, STATE, unit), F32), jax.ShapeDtypeStruct((size, rows, unit), F32)],
            [
                at_group((rows, unit)),
                at_group((count - 1, unit)),
                at_group((count, unit)),
                at_group((rows, STATE)),
                at_group((count - 1, STATE)),
                at_group((count, STATE)),
                at_lead((1, rows, per)),
                whole_map,
            ],
            [in_set((1, STATE, unit)), in_set((1, rows, unit))],
            (x_in, rim_x, conv_x, bc_in, rim_bc, conv_bc, tail, head_map),
        )

    def local(order, xc):
        size = order.shape[0]
        return call(
            local_kernel,
            order,
            [jax.ShapeDtypeStruct((size, rows, unit), F32)] * 2 + [jax.ShapeDtypeStruct((size, rows, STATE), F32)],
            [
                at_group((rows, STATE)),
                at_group((count - 1, STATE)),
                at_group((count, STATE)),
                at_group((rows, STATE), GROUPS),
                at_group((count - 1, STATE), GROUPS),
                at_group((count, STATE), GROUPS),
                in_set((1, rows, unit)),
                at_lead((1, rows, per)),
                at_lead((1, per, rows)),
                at_lead((1, rows + 8, per)),
                whole_map,
                at_group((rows, unit)),
            ],
            [in_set((1, rows, unit)), in_set((1, rows, unit)), in_set((1, rows, STATE))],
            (bc_in, rim_bc, conv_bc, bc_in, rim_bc, conv_bc, xc, cum, row, ecum, head_map, z_in),
        )

    def finish(order, before, c, m1, m2, out):
        spec = at_group((rows, unit))
        return call(
            finish_kernel,
            order,
            jax.ShapeDtypeStruct((rows, width), BF16),
            [
                in_set((1, STATE, unit)),
                in_set((1, rows, STATE)),
                in_set((1, rows, unit)),
                in_set((1, rows, unit)),
                at_group((1, unit)),
                pl.BlockSpec(memory_space=pl.ANY),
            ],
            spec,
            (before, c, m1, m2, gain[None], out),
            input_output_aliases={6: 0},
        )

    half = plane // 2
    sets = []
    for chunk in range(chunks):
        far = orders(chunk, range(half, plane))
        near = orders(chunk, range(half))
        sets.append((far, near))

    def upper(bit):
        return (j >> bit) & 1 == 1

    own_log, other_log = [], []
    for bit in range(bits):
        own_log.append(jnp.sum(logs[: 1 << bit], axis=0))
        other_log.append(jnp.sum(logs[1 << bit : 2 << bit], axis=0))

    levels, tops, top_rows, locals_ = [], [], [], []
    for chunk in range(chunks):
        far, near = sets[chunk]
        s_far, xc_far = states(far)
        s_near, xc_near = states(near)
        locals_.append(((far, xc_far), (near, xc_near)))
        keep, give = s_near, s_far
        stack = []
        for bit in range(bits):
            got = send(give, functools.partial(swap, bit=bit))
            order = orders(chunk, range(keep.shape[0]))
            lower_row = group_rows(jnp.where(upper(bit), other_log[bit], own_log[bit]), order)
            upper_row = group_rows(jnp.where(upper(bit), own_log[bit], other_log[bit]), order)
            lower_state = jnp.where(upper(bit), got, keep)
            upper_state = jnp.where(upper(bit), keep, got)
            both = lower_state * upper_row + upper_state
            stack.append((lower_row, lower_state))
            cut = both.shape[0] // 2
            keep, give = (both[:cut], both[cut:]) if cut else (both, None)
        levels.append(stack)
        tops.append(keep)
        top_rows.append(group_rows(jnp.sum(logs, axis=0), orders(chunk, [0])))

    pairs = [(i, i + plane) for i in range(n - plane)]
    entering = [jnp.zeros_like(tops[0])]
    for step in range(chunks + planes - 2 if planes > 1 else 0):
        which = jnp.clip(step - z, 0, chunks - 1)
        top, top_row = tops[0], top_rows[0]
        for chunk in range(1, chunks):
            top = jnp.where(which == chunk, tops[chunk], top)
            top_row = jnp.where(which == chunk, top_rows[chunk], top_row)
        entering.append(send(top_row * entering[-1] + top, lambda v: lax.ppermute(v, axis, pairs)))

    mixes = []
    for chunk in range(chunks):
        mixes.append([local(*one) for one in locals_[chunk]])

    out = pl.empty((rows, width), BF16) if False else jnp.zeros((rows, width), BF16)
    for chunk in range(chunks):
        state = entering[chunk]
        for at in range(1, planes):
            if chunk + at < len(entering):
                state = jnp.where(z == at, entering[chunk + at], state)
        state = jnp.where(z == 0, 0.0, state)
        other = None
        for bit in reversed(range(bits)):
            lower_row, lower_state = levels[chunk][bit]
            later = lower_row * state + lower_state
            other = send(jnp.where(upper(bit), state, later), functools.partial(swap, bit=bit))
            state = jnp.where(upper(bit), later, state)
            if bit:
                state = jnp.concatenate([state, other], axis=0)
        far, near = sets[chunk]
        m_far, m_near = mixes[chunk]
        out = finish(near, state, m_near[2], m_near[0], m_near[1], out)
        out = finish(far, other, m_far[2], m_far[0], m_far[1], out)
    return out


def solution(mesh):
    split_rows = P(("groups", "ctx"), None)
    return jax.shard_map(
        shards,
        mesh=mesh,
        in_specs=(split_rows,) * 4 + (P(),) * 6,
        out_specs=split_rows,
        check_vma=False,
    )
```

```python
import functools

import jax
import jax.numpy as jnp
from jax import lax
from jax.experimental import pallas as pl
from jax.experimental.pallas import tpu as pltpu
from jax.sharding import PartitionSpec as P

STATE = 128
GROUPS = 8
AXIS = "ctx"
EPS = 1e-05
VMEM_LIMIT = 16 * 2**20
F32, BF16 = jnp.float32, jnp.bfloat16
WIRE = jnp.float16
PEAK = 4 * 3.0 * 6.0
DT_TOP = 1.3133


def plane_size(n, groups):
    size = 1
    while (2 * size) ** 3 <= 4 * n and n % (2 * size) == 0 and groups % (2 * size) == 0:
        size *= 2
    return size


def silu(v):
    return v / (1.0 + jnp.exp(-v))


def split(v):
    hi = v.astype(BF16)
    return hi, (v - hi.astype(F32)).astype(BF16)


def mm(a, b, dims=((1,), (0,))):
    return lax.dot_general(a, b, (dims, ((), ())), preferred_element_type=F32)


def spread(v, e_ref):
    hi = v.astype(BF16)
    rest = v - hi.astype(F32)
    mid = rest.astype(BF16)
    low = (rest - mid.astype(F32)).astype(BF16)
    return mm(jnp.concatenate([hi, mid, low], axis=1), e_ref[...])


def conv_silu(x, halo, taps):
    count = taps.shape[0]
    xf = x.astype(F32)
    hf = halo.astype(F32)
    at = lax.broadcasted_iota(jnp.int32, (8, 1), 0)
    total = taps[count - 1 : count] * xf
    for back in range(1, count):
        moved = pltpu.roll(xf, back, 0)
        top = moved[:8]
        for row in range(back):
            src = hf.shape[0] - back + row
            top = jnp.where(at == row, hf[src : src + 1], top)
        moved = jnp.concatenate([top, moved[8:]], axis=0)
        total = total + taps[count - 1 - back : count - back] * moved
    return silu(total)


def ends_kernel(x_ref, bc_ref, out_ref):
    count, width = out_ref.shape[0], x_ref.shape[1]
    out_ref[:, :width] = x_ref[8 - count :]
    out_ref[:, width:] = bc_ref[8 - count :]


def load_kernel(*refs):
    count = (len(refs) - 1) // 2
    copies = [pltpu.make_async_copy(refs[k], refs[count + k], refs[-1].at[k]) for k in range(count)]
    for copy in copies:
        copy.start()
    for copy in copies:
        copy.wait()


def steps_kernel(dt_ref, bias_ref, rate_ref, skip_ref, tail_ref, cum_ref, row_ref, ecum_ref, tot_ref):
    groups, rows, per = tail_ref.shape
    v = dt_ref[...].astype(F32) + bias_ref[...]
    dt = jnp.maximum(v, 0.0) + jnp.log1p(jnp.exp(-jnp.abs(v)))
    cum = -rate_ref[...] * dt
    at = lax.broadcasted_iota(jnp.int32, cum.shape, 0)
    step = 1
    while step < rows:
        cum = cum + jnp.where(at >= step, pltpu.roll(cum, step, 0), 0.0)
        step *= 2
    total = cum[rows - 1 : rows]
    tot_ref[...] = total
    tail = jnp.exp(total - cum) * dt
    ecum = jnp.exp(cum)
    row = (jnp.log(dt) - cum).T
    for g in range(groups):
        cols = slice(g * per, (g + 1) * per)
        tail_ref[g] = tail[:, cols]
        cum_ref[g] = cum[:, cols]
        row_ref[g] = row[cols]
        ecum_ref[g, :rows] = ecum[:, cols]
        ecum_ref[g, rows:] = jnp.broadcast_to(skip_ref[:, cols], (8, per))


def reverse(p, bits):
    return sum(((p >> k) & 1) << (bits - 1 - k) for k in range(bits))


def my_place(plane):
    index = lax.axis_index(AXIS)
    return lax.rem(index, plane), lax.div(index, plane)


def rows_kernel(logs_ref, e_ref, tree_ref, chain_ref):
    chunks, plane, _, unit = tree_ref.shape
    bits = plane.bit_length() - 1
    per = e_ref.shape[0] // 3
    j, z = my_place(plane)
    logs = [logs_ref[r : r + 1] for r in range(plane)]
    rows, flags = [], []
    for bit in range(bits):
        own = sum(logs[1 : 1 << bit], logs[0])
        other = sum(logs[(1 << bit) + 1 : 2 << bit], logs[1 << bit])
        up = ((j >> bit) & 1) == 1
        none = jnp.zeros_like(own)
        rows += [
            jnp.where(up, none, other),
            jnp.where(up, own, none),
            jnp.where(up, none, own),
            none,
            jnp.where(up, other, none),
            none,
        ]
        flags += [1.0, 1.0, 1.0, jnp.where(up, 0.0, 1.0), 1.0, jnp.where(up, 1.0, 0.0)]
    rows.append(sum(logs[1:], logs[0]))
    flags.append(1.0)
    rows += [rows[-1]] * (-len(rows) % 8)
    decays = jnp.exp(jnp.concatenate(rows, axis=0))
    wide = [spread(decays[:, g * per : (g + 1) * per], e_ref) for g in range(chunks * plane)]
    for g in range(chunks * plane):
        at = reverse((g // chunks) ^ j, bits)
        for kind in range(6 * bits):
            tree_ref[g % chunks, at, kind : kind + 1] = wide[g][kind : kind + 1] * flags[kind]
    tops = []
    for chunk in range(chunks):
        top = wide[chunk][6 * bits : 6 * bits + 1]
        for q in range(1, plane):
            g = q * chunks + chunk
            top = jnp.where(j == q, wide[g][6 * bits : 6 * bits + 1], top)
        tops.append(top)
    one = jnp.ones((1, unit), F32)
    planes, moves = chain_shape(plane, chunks)
    at = 0
    for step in range(moves):
        total = jnp.zeros_like(one)
        for chunk in range(chunks):
            here = jnp.where(step - z == chunk, 1.0, 0.0)
            total = total + tops[chunk] * here
            chain_ref[at + 1 + chunk] = one * here
        chain_ref[at] = total
        at += 1 + chunks
    for here in range(planes):
        chain_ref[at + here] = one * jnp.where(z == here, 1.0, 0.0)


def chain_shape(plane, chunks):
    planes = lax.axis_size(AXIS) // plane
    return planes, chunks + planes - 2 if planes > 1 else 0


def group_at(p, chunk, chunks, bits):
    return (reverse(p, bits) ^ my_place(1 << bits)[0]) * chunks + chunk


def lanes(at, size):
    return pl.ds(pl.multiple_of(at * size, size), size)


def state_kernel(place, token_ref, x_ref, rim_ref, tx_ref, b_ref, tb_ref, tail_ref, e_ref, s_ref, xc_ref):
    chunk, base, size, chunks, bits = place
    unit = e_ref.shape[1]
    for k in range(size):
        g = group_at(base + k, chunk, chunks, bits)
        at, at_b = lanes(g, unit), lanes(g, STATE)
        at_rim = lanes(g + x_ref.shape[1] // STATE, STATE)
        xc = conv_silu(x_ref[:, at], rim_ref[:, at], tx_ref[:, at])
        xc_ref[k] = xc
        b = conv_silu(b_ref[:, at_b], rim_ref[:, at_rim], tb_ref[:, at_b])
        xt = xc * spread(tail_ref[g], e_ref)
        xhi, xlo = split(xt)
        bhi, blo = split(b)
        s = mm(jnp.concatenate([bhi, blo], axis=0), jnp.concatenate([xhi, xhi], axis=0), ((0,), (0,)))
        s_ref[k] = s + mm(bhi, xlo, ((0,), (0,)))


def local_kernel(place, token_ref, b_ref, rim_ref, tb_ref, xc_ref, cum_ref, row_ref, ecum_ref, e_ref, z_ref, m1_ref, m2_ref, co_ref):
    chunk, base, size, chunks, bits = place
    unit = e_ref.shape[1]
    rows = z_ref.shape[0]
    per = cum_ref.shape[2]
    hdim = unit // per
    causal = lax.broadcasted_iota(jnp.int32, (rows, rows), 0) >= lax.broadcasted_iota(jnp.int32, (rows, rows), 1)
    first = lax.broadcasted_iota(jnp.int32, (rows, 2 * hdim), 1) < hdim
    last = ((1,), (1,))
    for k in range(size):
        g = group_at(base + k, chunk, chunks, bits)
        at = lanes(g, unit)
        pair_bc = []
        for more in (0, GROUPS):
            at_b = lanes(g + more, STATE)
            at_rim = lanes(g + more + z_ref.shape[1] // STATE, STATE)
            pair_bc.append(conv_silu(b_ref[:, at_b], rim_ref[:, at_rim], tb_ref[:, at_b]))
        b, c = pair_bc
        co_ref[k] = c
        bhi, blo = split(b)
        chi, clo = split(c)
        scores = mm(jnp.concatenate([chi, clo], axis=1), jnp.concatenate([bhi, bhi], axis=1), last) + mm(chi, blo, last)
        wide = spread(ecum_ref[g], e_ref)
        z = silu(z_ref[:, at].astype(F32))
        m1_ref[k] = wide[:rows] * z
        skip = wide[rows : rows + 1]
        for pair in range(per // 2):
            cols = slice(pair * 2 * hdim, (pair + 1) * 2 * hdim)
            weights = []
            for h in (2 * pair, 2 * pair + 1):
                e = jnp.exp(cum_ref[g, :, h : h + 1] + row_ref[g, h : h + 1, :])
                weights.append(jnp.where(causal, e * scores, 0.0))
            w = jnp.concatenate(weights, axis=1)
            x = xc_ref[k, :, cols]
            xb = jnp.concatenate([jnp.where(first, x, 0.0), jnp.where(first, 0.0, x)], axis=0)
            whi, wlo = split(w)
            xhi, xlo = split(xb)
            y = mm(whi, xhi) + mm(wlo, xhi) + mm(whi, xlo)
            m2_ref[k, :, cols] = (y + skip[:, cols] * x) * z[:, cols]


def finish_kernel(place, token_ref, p_ref, c_ref, m1_ref, m2_ref, gain_ref, *refs):
    chunk, base, size, chunks, bits = place
    out_ref, done_ref, sem = refs[-3:]
    unit = p_ref.shape[2]
    copies = []
    for k in range(size):
        at = lanes(group_at(base + k, chunk, chunks, bits), unit)
        chi, clo = split(c_ref[k])
        phi, plo = split(p_ref[k])
        y = mm(jnp.concatenate([chi, clo], axis=1), jnp.concatenate([phi, phi], axis=0)) + mm(chi, plo)
        gated = m2_ref[k] + m1_ref[k] * y
        scale = lax.rsqrt(jnp.mean(gated * gated, axis=1, keepdims=True) + EPS)
        done_ref[k] = (gated * scale * gain_ref[:, at]).astype(BF16)
        copies.append(pltpu.make_async_copy(done_ref.at[k], out_ref.at[:, at], sem.at[k]))
        copies[-1].start()
    for copy in copies:
        copy.wait()


def shards(x_in, bc_in, z_in, dt_in, conv_x, conv_bc, dt_bias, a_rate, d_skip, gain):
    rows, width = x_in.shape
    heads = dt_bias.shape[0]
    hdim = width // heads
    per = heads // GROUPS
    unit = per * hdim
    gain = gain[None]
    x_in, bc_in, z_in, conv_x, conv_bc, gain = [
        pltpu.with_memory_space_constraint(v, pltpu.HBM) for v in (x_in, bc_in, z_in, conv_x, conv_bc, gain)
    ]
    count = conv_x.shape[0]
    axis = AXIS
    n = lax.axis_size(axis)
    plane = plane_size(n, GROUPS)
    planes = n // plane
    chunks = GROUPS // plane
    bits = plane.bit_length() - 1
    half = plane // 2
    scale = 2.0 ** -max(0, 1 + int(n * rows * DT_TOP * PEAK * PEAK / 65504.0).bit_length())
    small_vmem = pltpu.CompilerParams(vmem_limit_bytes=VMEM_LIMIT)
    in_vmem = pl.BlockSpec(memory_space=pltpu.VMEM)
    in_hbm = pl.BlockSpec(memory_space=pltpu.HBM)

    def near(v):
        return pltpu.with_memory_space_constraint(v, pltpu.VMEM)

    def swap(v, bit):
        return lax.ppermute(v, axis, [(i, i ^ (1 << bit)) for i in range(n)])

    def pack(v):
        return (v * scale).astype(WIRE)

    def unpack(v):
        return v.astype(F32) * (1.0 / scale)

    last = rows // 8 - 1
    ends = pl.pallas_call(
        ends_kernel,
        grid=(1,),
        out_shape=jax.ShapeDtypeStruct((count - 1, width + bc_in.shape[1]), BF16),
        in_specs=[
            pl.BlockSpec((8, width), lambda s: (last, 0)),
            pl.BlockSpec((8, bc_in.shape[1]), lambda s: (last, 0)),
        ],
        out_specs=pl.BlockSpec((count - 1, width + bc_in.shape[1]), lambda s: (0, 0)),
        compiler_params=small_vmem,
    )(x_in, bc_in)
    rim = near(lax.ppermute(ends, axis, [(i, i + 1) for i in range(n - 1)]))
    held = (x_in, bc_in, z_in, conv_x, conv_bc, gain)
    x_in, bc_in, z_in, conv_x, conv_bc, gain = pl.pallas_call(
        load_kernel,
        out_shape=[pltpu.VMEM(v.shape, v.dtype) for v in held],
        in_specs=[pl.BlockSpec(memory_space=pltpu.HBM)] * len(held),
        out_specs=[in_vmem] * len(held),
        scratch_shapes=[pltpu.SemaphoreType.DMA((len(held),))],
        compiler_params=small_vmem,
    )(*held)

    small = [
        pltpu.VMEM((GROUPS, rows, per), F32),
        pltpu.VMEM((GROUPS, rows, per), F32),
        pltpu.VMEM((GROUPS, per, rows), F32),
        pltpu.VMEM((GROUPS, rows + 8, per), F32),
        jax.ShapeDtypeStruct((1, heads), F32),
    ]
    tail, cum, row, ecum, total = pl.pallas_call(
        steps_kernel,
        out_shape=small,
        out_specs=[in_vmem] * len(small),
        compiler_params=small_vmem,
    )(dt_in, dt_bias[None], a_rate[None], d_skip[None])
    token = near(total)
    logs = total
    for bit in range(bits):
        logs = jnp.concatenate([logs, swap(logs, bit)], axis=0)

    head_map = (jnp.arange(unit)[None, :] // hdim == jnp.arange(per)[:, None]).astype(BF16)
    head_map = near(jnp.concatenate([head_map] * 3, axis=0))
    moves = chain_shape(plane, chunks)[1]
    tree, chain = pl.pallas_call(
        rows_kernel,
        out_shape=[
            pltpu.VMEM((chunks, plane, 6 * bits, unit), F32),
            pltpu.VMEM((moves * (1 + chunks) + planes, 1, unit), F32),
        ],
        in_specs=[in_vmem] * 2,
        out_specs=[in_vmem] * 2,
        compiler_params=small_vmem,
    )(near(logs), head_map)

    def factor(chunk, size, bit, kind):
        return tree[chunk, :size, 6 * bit + kind][:, None]

    def tie(value, *others):
        return lax.optimization_barrier((value, *others))[0] if others else value

    def call(body, place, outs, args, after):
        return pl.pallas_call(
            functools.partial(body, (*place, chunks, bits)),
            out_shape=[pltpu.VMEM(*o) for o in outs],
            in_specs=[in_vmem] * (1 + len(args)),
            out_specs=[in_vmem] * len(outs),
            compiler_params=small_vmem,
        )(tie(token, *after), *args)

    def states(*place, after=()):
        size = place[2]
        outs = [((size, STATE, unit), F32), ((size, rows, unit), F32)]
        return call(state_kernel, place, outs, (x_in, rim, conv_x, bc_in, conv_bc, tail, head_map), after)

    def local(*place, xc, after=()):
        size = place[2]
        outs = [((size, rows, unit), F32)] * 2 + [((size, rows, STATE), F32)]
        return call(local_kernel, place, outs, (bc_in, rim, conv_bc, xc, cum, row, ecum, head_map, z_in), after)

    def finish(*place, before, mixed, out):
        size = place[2]
        m1, m2, c = mixed
        kept = () if out is None else (out,)
        return pl.pallas_call(
            functools.partial(finish_kernel, (*place, chunks, bits)),
            out_shape=jax.ShapeDtypeStruct((rows, width), BF16),
            in_specs=[in_vmem] * 6 + [in_hbm] * len(kept),
            out_specs=in_hbm,
            scratch_shapes=[pltpu.VMEM((size, rows, unit), BF16), pltpu.SemaphoreType.DMA((size,))],
            input_output_aliases={6: 0} if kept else {},
            compiler_params=small_vmem,
        )(token, near(before), c, m1, m2, gain, *kept)

    levels = [[] for _ in range(chunks)]
    tops, pieces = [], []

    def climb(chunk, keep, wire, bit):
        levels[chunk].append((keep, wire))
        size = keep.shape[0]
        return keep * factor(chunk, size, bit, 0) + unpack(wire) * factor(chunk, size, bit, 1)

    gate = ()
    for chunk in range(chunks):
        s_far, xc_far = states(chunk, half, half, after=gate)
        give = pack(s_far)
        wire = swap(give, 0)
        s_near, xc_near = states(chunk, 0, half, after=(give,))
        pieces += [(chunk, half, xc_far), (chunk, 0, xc_near)]
        both = climb(chunk, s_near, wire, 0)
        for bit in range(1, bits):
            cut = both.shape[0] // 2
            keep, give = both[:cut], pack(both[cut:])
            gate = (give,)
            both = climb(chunk, keep, swap(give, bit), bit)
        tops.append(lax.optimization_barrier(both))

    pairs = [(i, i + plane) for i in range(n - plane)]
    entering = [jnp.zeros((1, STATE, unit), WIRE)]
    mixes = {}

    def work(number, *after):
        for _ in range(number):
            if len(mixes) < len(pieces):
                chunk, base, xc = pieces[len(mixes)]
                mixes[chunk, base] = local(chunk, base, half, xc=xc, after=after)

    for step in range(moves):
        at = step * (1 + chunks)
        value = unpack(entering[-1]) * chain[at] if step else 0.0
        for chunk in range(max(0, step - planes + 1), min(chunks - 1, step) + 1):
            value = value + tops[chunk] * chain[at + 1 + chunk]
        give = pack(value)
        wire = lax.ppermute(give, axis, pairs)
        if step:
            done = len(mixes)
            work(1, give)
            if len(mixes) > done:
                wire = tie(wire, list(mixes.values())[-1][2])
        entering.append(wire)
    work(len(pieces))

    out = None
    for chunk in range(chunks):
        state = 0.0
        for at in range(1, planes):
            if chunk + at < len(entering):
                state = state + unpack(entering[chunk + at]) * chain[moves * (1 + chunks) + at]
        other = None
        for bit in reversed(range(bits)):
            keep, got = levels[chunk][bit]
            size = keep.shape[0]
            give = pack(state * factor(chunk, size, bit, 2) + keep * factor(chunk, size, bit, 3))
            other = unpack(swap(give, bit))
            state = state * factor(chunk, size, bit, 4) + unpack(got) * factor(chunk, size, bit, 5)
            if bit:
                state = jnp.concatenate([state, other], axis=0)
        out = finish(chunk, 0, half, before=state, mixed=mixes[chunk, 0], out=out)
        out = finish(chunk, half, half, before=other, mixed=mixes[chunk, half], out=out)
    return out


def solution(mesh):
    split_rows = P(("groups", "ctx"), None)
    return jax.shard_map(
        shards,
        mesh=mesh,
        in_specs=(split_rows,) * 4 + (P(),) * 6,
        out_specs=split_rows,
        check_vma=False,
    )
```
